32 devices in a mesh: seq: 4 (over y, x), ctx: 8 (over z, core).
Axes of the slice: x: 2, y: 2, z: 4, core: 2. Of those that a mesh axis runs over, the one named last changes fastest.
Arguments:
- inputs: bfloat16 [4096, 1152], P(('seq', 'ctx')), may hold values from -140 to 140
- positions: int32 [4096], P(('seq', 'ctx')), may hold values from 0 to 1023, as said below
- attention_gain: bfloat16 [1152], P(('seq', 'ctx')), may hold values from 0.3984375 to 1.59375
- query_weight: bfloat16 [1152, 1024], P(('seq', 'ctx')), may hold values from -0.1875 to 0.1875
- key_weight: bfloat16 [1152, 256], P(('seq', 'ctx')), may hold values from -0.1875 to 0.1875
- value_weight: bfloat16 [1152, 256], P(('seq', 'ctx')), may hold values from -0.1875 to 0.1875
- query_gain: bfloat16 [256], P(('seq', 'ctx')), may hold values from 0.5 to 1.5
- key_gain: bfloat16 [256], P(('seq', 'ctx')), may hold values from 0.5 to 1.5
- output_weight: bfloat16 [1024, 1152], P(('seq', 'ctx')), may hold values from -0.1875 to 0.1875
- attention_post: bfloat16 [1152], P(('seq', 'ctx')), may hold values from 0.3984375 to 1.59375
- feedfwd_gain: bfloat16 [1152], P(('seq', 'ctx')), may hold values from 0.3984375 to 1.59375
- gate_weight: bfloat16 [1152, 6912], P(('seq', 'ctx')), may hold values from -0.1875 to 0.1875
- up_weight: bfloat16 [1152, 6912], P(('seq', 'ctx')), may hold values from -0.1875 to 0.1875
- down_weight: bfloat16 [6912, 1152], P(('seq', 'ctx')), may hold values from -0.078125 to 0.078125
- feedfwd_post: bfloat16 [1152], P(('seq', 'ctx')), may hold values from 0.3984375 to 1.59375
- cotangent: bfloat16 [4096, 1152], P(('seq', 'ctx')), may hold values from -6 to 6
Outputs:
- block_out: bfloat16 [4096, 1152], P(('seq', 'ctx'))
- input_grad: float32 [4096, 1152], P(('seq', 'ctx'))
- attention_gain_grad: float32 [1152], P(('seq', 'ctx'))
- query_grad: float32 [1152, 1024], P(('seq', 'ctx'))
- key_grad: float32 [1152, 256], P(('seq', 'ctx'))
- value_grad: float32 [1152, 256], P(('seq', 'ctx'))
- query_gain_grad: float32 [256], P(('seq', 'ctx'))
- key_gain_grad: float32 [256], P(('seq', 'ctx'))
- output_grad: float32 [1024, 1152], P(('seq', 'ctx'))
- attention_post_grad: float32 [1152], P(('seq', 'ctx'))
- feedfwd_gain_grad: float32 [1152], P(('seq', 'ctx'))
- gate_grad: float32 [1152, 6912], P(('seq', 'ctx'))
- up_grad: float32 [1152, 6912], P(('seq', 'ctx'))
- down_grad: float32 [6912, 1152], P(('seq', 'ctx'))
- feedfwd_post_grad: float32 [1152], P(('seq', 'ctx'))
The draws below stay inside these ranges and needn't reach their ends.
Inputs may be any that keep to these rules, and one draw needn't show every extreme that they name: Within each sequence of 1024 tokens, the 128 tokens of each ctx index hold the consecutive positions k * 128 to k * 128 + 127, where the block numbers k of one sequence's ctx indices are a permutation of 0 to 7, drawn afresh for every sequence.
All inputs are finite; a program needn't handle non-finite values.
Results may differ from the reference program's by a relative error of at most 0.038.
Values may be sent and summed in bfloat16 or wider, within the bound.
A program may use at most 448 MiB of HBM per device.

```python
import math
import jax
import jax.numpy as jnp
from jax import lax

D = 1152
H = 4
DH = 256
FF = 6912
TOK_DEV = 128
LENGTH = 1024
SEQS = 4
TOKENS = 4096


def draw_positions(key, part):
    block_total = LENGTH // TOK_DEV
    subkeys = jax.random.split(key, SEQS)
    orders = jax.vmap(lambda subkey: jax.random.permutation(subkey, block_total))(subkeys)
    offsets = jnp.arange(TOK_DEV, dtype=jnp.int32)
    table = orders.astype(jnp.int32)[:, :, None] * TOK_DEV + offsets[None, None, :]
    return table.reshape(TOKENS)


def draw_inputs(key, part):
    key_base, key_rows, key_cols, key_pair = jax.random.split(jax.random.fold_in(key, 7), 4)
    device_total = TOKENS // TOK_DEV
    base = jax.random.truncated_normal(key_base, -3.0, 3.0, (TOKENS, D), jnp.float32)
    row_scale = jnp.exp(jax.random.uniform(key_rows, (TOKENS, 1), jnp.float32, math.log(0.3), math.log(3.0)))
    col_scale = jnp.exp(jax.random.uniform(key_cols, (1, D), jnp.float32, math.log(0.3), math.log(3.0)))
    pairing = jax.random.permutation(key_pair, device_total)
    row_block = jnp.arange(TOKENS, dtype=jnp.int32) // TOK_DEV
    col_block = jnp.arange(D, dtype=jnp.int32) // (D // device_total)
    spiked = col_block[None, :] == pairing[row_block][:, None]
    values = base * row_scale * col_scale * jnp.where(spiked, 2.5, 1.0)
    return values.astype(jnp.bfloat16)


def level_of(stream_key, shape, cuts, least, top_value):
    def one(position, blocks):
        heights = jax.random.uniform(jax.random.fold_in(jax.random.fold_in(stream_key, 6), position), (blocks,), jnp.float32, least / len(cuts), top_value / len(cuts))
        return jnp.repeat(jnp.exp(heights), shape[position] // blocks).reshape((-1,) + (1,) * (len(shape) - position - 1))

    loudness = one(*cuts[0])
    for cut in cuts[1:]:
        loudness = loudness * one(*cut)
    return loudness


def noise(key, shape, deviation, most, cuts=(), held_as=jnp.bfloat16):
    level = level_of(key, shape, cuts, -0.22, 0.18) if cuts else 1.0
    result = jax.random.normal(key, shape, jnp.float32) * deviation * level
    return jnp.minimum(jnp.maximum(result, -most), most).astype(held_as)


def setup_inputs(seed: int = 0) -> dict:
    key_of = jax.random.split(jax.random.key(seed), 17)
    return {
        "inputs": draw_inputs(jax.random.fold_in(key_of[16], 71), 0),
        "positions": draw_positions(jax.random.fold_in(key_of[16], 71), 0),
        "attention_gain": jnp.clip(1.0 + 0.12 * jax.random.normal(key_of[2], (D,), jnp.float32), 0.3984375, 1.59375).astype(jnp.bfloat16),
        "query_weight": noise(key_of[3], (D, H * DH), D ** -0.5, 0.1875, ((0, 32),)),
        "key_weight": noise(key_of[4], (D, DH), D ** -0.5, 0.1875, ((0, 32),)),
        "value_weight": noise(key_of[5], (D, DH), D ** -0.5, 0.1875, ((0, 32),)),
        "query_gain": jnp.clip(1.0 + 0.1 * jax.random.normal(key_of[6], (DH,), jnp.float32), 0.5, 1.5).astype(jnp.bfloat16),
        "key_gain": jnp.clip(1.0 + 0.1 * jax.random.normal(key_of[7], (DH,), jnp.float32), 0.5, 1.5).astype(jnp.bfloat16),
        "output_weight": noise(key_of[8], (H * DH, D), (H * DH) ** -0.5, 0.1875, ((0, 32),)),
        "attention_post": jnp.clip(1.0 + 0.12 * jax.random.normal(key_of[9], (D,), jnp.float32), 0.3984375, 1.59375).astype(jnp.bfloat16),
        "feedfwd_gain": jnp.clip(1.0 + 0.12 * jax.random.normal(key_of[10], (D,), jnp.float32), 0.3984375, 1.59375).astype(jnp.bfloat16),
        "gate_weight": noise(key_of[11], (D, FF), D ** -0.5, 0.1875, ((0, 32),)),
        "up_weight": noise(key_of[12], (D, FF), D ** -0.5, 0.1875, ((0, 32),)),
        "down_weight": noise(key_of[13], (FF, D), FF ** -0.5, 0.078125, ((0, 32),)),
        "feedfwd_post": jnp.clip(1.0 + 0.12 * jax.random.normal(key_of[14], (D,), jnp.float32), 0.3984375, 1.59375).astype(jnp.bfloat16),
        "cotangent": noise(key_of[15], (TOKENS, D), 1.0, 6.0, ((0, 32),)),
    }


EPSILON = 1e-06
THETA = 1000000.0
GELU_COEF = math.sqrt(2.0 / math.pi)

def rounded(values):
    return lax.optimization_barrier(values.astype(jnp.bfloat16))

def widened(values):
    return values.astype(jnp.float32)

def rms_factor(values):
    return lax.rsqrt(lax.optimization_barrier(jnp.mean(values * values, axis=-1, keepdims=True)) + EPSILON)

def norm_back(values, factor, gain_vector, upstream):
    scaled = gain_vector * upstream
    cubed = factor * factor * factor
    return factor * scaled - values * cubed * lax.optimization_barrier(jnp.mean(scaled * values, axis=-1, keepdims=True))

def rotary(places):
    half_width = DH // 2
    exponent = jnp.arange(half_width, dtype=jnp.float32) * (-2.0 / DH)
    frequency = jnp.power(jnp.float32(THETA), exponent)
    angles = places.astype(jnp.float32)[:, None] * frequency[None, :]
    return (jnp.cos(angles), jnp.sin(angles))

def rotate(values, cosine, sinus):
    half_width = values.shape[-1] // 2
    first = values[..., :half_width]
    second = values[..., half_width:]
    return jnp.concatenate([first * cosine - second * sinus, second * cosine + first * sinus], axis=-1)

def rotate_back(upstream, cosine, sinus):
    half_width = upstream.shape[-1] // 2
    first = upstream[..., :half_width]
    second = upstream[..., half_width:]
    return jnp.concatenate([first * cosine + second * sinus, second * cosine - first * sinus], axis=-1)

def gelu_tanh(values):
    inner = GELU_COEF * (values + 0.044715 * values * values * values)
    return 0.5 * values * (1.0 + jnp.tanh(inner))

def gelu_slope(values):
    inner = GELU_COEF * (values + 0.044715 * values * values * values)
    tangent = jnp.tanh(inner)
    return 0.5 * (1.0 + tangent) + 0.5 * values * (1.0 - tangent * tangent) * GELU_COEF * (1.0 + 3.0 * 0.044715 * values * values)

def times_right(left_side, right_side):
    return jnp.dot(left_side, right_side, preferred_element_type=jnp.float32)

def times_transposed(left_side, right_side):
    return lax.dot_general(left_side, right_side, (((1,), (1,)), ((), ())), preferred_element_type=jnp.float32)

def transposed_times(left_side, right_side):
    return lax.dot_general(left_side, right_side, (((0,), (0,)), ((), ())), preferred_element_type=jnp.float32)

def attend(query_part, place_part, key_rot, value_rows, key_places):
    scaling = 1.0 / math.sqrt(DH)
    scores = jnp.einsum('qhd,kd->hqk', widened(query_part), widened(key_rot)) * scaling
    allowed = key_places[None, None, :] <= place_part[None, :, None]
    expscore = jnp.where(allowed, jnp.exp(scores), 0.0)
    weight_sum = lax.optimization_barrier(jnp.sum(expscore, axis=-1))
    summed = jnp.einsum('hqk,kd->qhd', widened(rounded(expscore)), widened(value_rows))
    attended = rounded(summed / jnp.transpose(weight_sum)[:, :, None])
    return (attended, jnp.transpose(jnp.log(weight_sum)))

def attend_back(query_part, place_part, output_part, logsum_part, upper_part, key_rot, value_rows, key_places):
    scaling = 1.0 / math.sqrt(DH)
    upper_round = widened(rounded(upper_part))
    row_delta = lax.optimization_barrier(jnp.sum(upper_part * widened(output_part), axis=-1))
    scores = jnp.einsum('qhd,kd->hqk', widened(query_part), widened(key_rot)) * scaling
    allowed = key_places[None, None, :] <= place_part[None, :, None]
    probability = jnp.where(allowed, jnp.exp(scores - jnp.transpose(logsum_part)[:, :, None]), 0.0)
    value_sum = jnp.einsum('hqk,qhd->kd', widened(rounded(probability)), upper_round)
    prob_back = jnp.einsum('qhd,kd->hqk', upper_round, widened(value_rows))
    score_back = widened(rounded(probability * (prob_back - jnp.transpose(row_delta)[:, :, None]) * scaling))
    query_back = jnp.einsum('hqk,kd->qhd', score_back, widened(key_rot))
    key_back = jnp.einsum('hqk,qhd->kd', score_back, widened(query_part))
    return (query_back, key_back, value_sum)

def reference(inputs, positions, attention_gain, query_weight, key_weight, value_weight, query_gain, key_gain, output_weight, attention_post, feedfwd_gain, gate_weight, up_weight, down_weight, feedfwd_post, cotangent):
    gain_attention = widened(attention_gain)
    gain_query = widened(query_gain)
    gain_key = widened(key_gain)
    gain_post = widened(attention_post)
    gain_feed = widened(feedfwd_gain)
    gain_final = widened(feedfwd_post)
    block_len = min(LENGTH, 512)
    block_count = LENGTH // block_len

    def one_sequence(grad_state, packet):
        seq_inputs, seq_places, seq_cot = packet
        input_wide = widened(seq_inputs)
        input_factor = rms_factor(input_wide)
        normed = rounded(input_wide * input_factor * gain_attention)
        queries = times_right(normed, query_weight).reshape(LENGTH, H, DH)
        key_rows = times_right(normed, key_weight)
        value_rows = rounded(times_right(normed, value_weight))
        cosine, sinus = rotary(seq_places)
        query_factor = rms_factor(queries)
        query_rot = rounded(rotate(queries * query_factor * gain_query, cosine[:, None, :], sinus[:, None, :]))
        key_factor = rms_factor(key_rows)
        key_rot = rounded(rotate(key_rows * key_factor * gain_key, cosine, sinus))
        query_blocks = query_rot.reshape(block_count, block_len, H, DH)
        place_blocks = seq_places.reshape(block_count, block_len)
        attended_blocks, logsum_blocks = lax.map(lambda pair: attend(pair[0], pair[1], key_rot, value_rows, seq_places), (query_blocks, place_blocks))
        attended = attended_blocks.reshape(LENGTH, H * DH)
        mixed_values = times_right(attended, output_weight)
        mixed_factor = rms_factor(mixed_values)
        residual = input_wide + mixed_values * mixed_factor * gain_post
        residual_factor = rms_factor(residual)
        fed_rows = rounded(residual * residual_factor * gain_feed)
        gate_values = times_right(fed_rows, gate_weight)
        up_values = times_right(fed_rows, up_weight)
        hidden = rounded(gelu_tanh(gate_values) * up_values)
        down_values = times_right(hidden, down_weight)
        down_factor = rms_factor(down_values)
        block_out = rounded(residual + down_values * down_factor * gain_final)
        cot_wide = widened(seq_cot)
        grad_final = lax.optimization_barrier(jnp.sum(cot_wide * down_values * down_factor, axis=0))
        down_back = rounded(norm_back(down_values, down_factor, gain_final, cot_wide))
        grad_down = transposed_times(hidden, down_back)
        hidden_back = times_transposed(down_back, down_weight)
        gate_back = rounded(hidden_back * up_values * gelu_slope(gate_values))
        up_back = rounded(hidden_back * gelu_tanh(gate_values))
        grad_gate = transposed_times(fed_rows, gate_back)
        grad_up = transposed_times(fed_rows, up_back)
        fed_back = times_transposed(gate_back, gate_weight) + times_transposed(up_back, up_weight)
        grad_feed = lax.optimization_barrier(jnp.sum(fed_back * residual * residual_factor, axis=0))
        residual_back = cot_wide + norm_back(residual, residual_factor, gain_feed, fed_back)
        grad_post = lax.optimization_barrier(jnp.sum(residual_back * mixed_values * mixed_factor, axis=0))
        mixed_back = rounded(norm_back(mixed_values, mixed_factor, gain_post, residual_back))
        grad_output = transposed_times(attended, mixed_back)
        attended_back = times_transposed(mixed_back, output_weight).reshape(LENGTH, H, DH)

        def back_block(state_now, pieces):
            query_part, place_part, output_part, logsum_part, upper_part = pieces
            query_back, key_back, value_sum = attend_back(query_part, place_part, output_part, logsum_part, upper_part, key_rot, value_rows, seq_places)
            return ((state_now[0] + key_back, state_now[1] + value_sum), query_back)
        zero_rows = jnp.zeros((LENGTH, DH), jnp.float32)
        (key_rot_back, value_sum), query_parts = lax.scan(back_block, (zero_rows, zero_rows), (query_blocks, place_blocks, attended_blocks, logsum_blocks, attended_back.reshape(block_count, block_len, H, DH)))
        query_rot_back = query_parts.reshape(LENGTH, H, DH)
        query_up = rotate_back(query_rot_back, cosine[:, None, :], sinus[:, None, :])
        grad_qgain = lax.optimization_barrier(jnp.sum(query_up * queries * query_factor, axis=(0, 1)))
        query_back = rounded(norm_back(queries, query_factor, gain_query, query_up)).reshape(LENGTH, H * DH)
        key_up = rotate_back(key_rot_back, cosine, sinus)
        grad_kgain = lax.optimization_barrier(jnp.sum(key_up * key_rows * key_factor, axis=0))
        key_back = rounded(norm_back(key_rows, key_factor, gain_key, key_up))
        value_back = rounded(value_sum)
        grad_query = transposed_times(normed, query_back)
        grad_key = transposed_times(normed, key_back)
        grad_value = transposed_times(normed, value_back)
        normed_back = times_transposed(query_back, query_weight) + times_transposed(key_back, key_weight) + times_transposed(value_back, value_weight)
        grad_attention = lax.optimization_barrier(jnp.sum(normed_back * input_wide * input_factor, axis=0))
        input_grad = residual_back + norm_back(input_wide, input_factor, gain_attention, normed_back)
        terms = (grad_attention, grad_query, grad_key, grad_value, grad_qgain, grad_kgain, grad_output, grad_post, grad_feed, grad_gate, grad_up, grad_down, grad_final)
        updated = tuple((before + term for before, term in zip(grad_state, terms)))
        return (updated, (block_out, input_grad))
    initial = (jnp.zeros((D,), jnp.float32), jnp.zeros((D, H * DH), jnp.float32), jnp.zeros((D, DH), jnp.float32), jnp.zeros((D, DH), jnp.float32), jnp.zeros((DH,), jnp.float32), jnp.zeros((DH,), jnp.float32), jnp.zeros((H * DH, D), jnp.float32), jnp.zeros((D,), jnp.float32), jnp.zeros((D,), jnp.float32), jnp.zeros((D, FF), jnp.float32), jnp.zeros((D, FF), jnp.float32), jnp.zeros((FF, D), jnp.float32), jnp.zeros((D,), jnp.float32))
    packets = (inputs.reshape(SEQS, LENGTH, D), positions.reshape(SEQS, LENGTH), cotangent.reshape(SEQS, LENGTH, D))
    grads_all, (outputs_all, input_grads) = lax.scan(one_sequence, initial, packets)
    return (outputs_all.reshape(TOKENS, D), input_grads.reshape(TOKENS, D), grads_all[0], grads_all[1], grads_all[2], grads_all[3], grads_all[4], grads_all[5], grads_all[6], grads_all[7], grads_all[8], grads_all[9], grads_all[10], grads_all[11], grads_all[12])
```

```python
import math

import jax
import jax.numpy as jnp
from jax import lax
from jax.sharding import PartitionSpec as P

D = 1152
H = 4
DH = 256
FF = 6912


EPSILON = 1e-06
THETA = 1000000.0
GELU_COEF = math.sqrt(2.0 / math.pi)


def rms_factor(values):
    return lax.rsqrt(jnp.mean(values * values, axis=-1, keepdims=True) + EPSILON)


def norm_back(values, factor, gain_vector, upstream):
    scaled = gain_vector * upstream
    cubed = factor * factor * factor
    return factor * scaled - values * cubed * jnp.mean(scaled * values, axis=-1, keepdims=True)


def rotary(places):
    half_width = DH // 2
    exponent = jnp.arange(half_width, dtype=jnp.float32) * (-2.0 / DH)
    frequency = jnp.power(jnp.float32(THETA), exponent)
    angles = places.astype(jnp.float32)[:, None] * frequency[None, :]
    return (jnp.cos(angles), jnp.sin(angles))


def rotate(values, cosine, sinus):
    half_width = values.shape[-1] // 2
    first = values[..., :half_width]
    second = values[..., half_width:]
    return jnp.concatenate(
        [first * cosine - second * sinus, second * cosine + first * sinus], axis=-1
    )


def rotate_back(upstream, cosine, sinus):
    half_width = upstream.shape[-1] // 2
    first = upstream[..., :half_width]
    second = upstream[..., half_width:]
    return jnp.concatenate(
        [first * cosine + second * sinus, second * cosine - first * sinus], axis=-1
    )


def gelu_tanh(values):
    inner = GELU_COEF * (values + 0.044715 * values * values * values)
    return 0.5 * values * (1.0 + jnp.tanh(inner))


def gelu_slope(values):
    inner = GELU_COEF * (values + 0.044715 * values * values * values)
    tangent = jnp.tanh(inner)
    return 0.5 * (1.0 + tangent) + 0.5 * values * (1.0 - tangent * tangent) * GELU_COEF * (
        1.0 + 3.0 * 0.044715 * values * values
    )


def times_right(left_side, right_side):
    return jnp.dot(left_side, right_side, preferred_element_type=jnp.float32)


def times_transposed(left_side, right_side):
    return lax.dot_general(
        left_side, right_side, (((1,), (1,)), ((), ())), preferred_element_type=jnp.float32
    )


def transposed_times(left_side, right_side):
    return lax.dot_general(
        left_side, right_side, (((0,), (0,)), ((), ())), preferred_element_type=jnp.float32
    )


BOTH = ("seq", "ctx")


def to_heads(rows):
    return jnp.concatenate([rows[:, h * DH : (h + 1) * DH] for h in range(H)], axis=0)


def from_heads(stacked):
    count = stacked.shape[0] // H
    return jnp.concatenate([stacked[h * count : (h + 1) * count] for h in range(H)], axis=1)


def sum_to_owner(term):
    columns = term.shape[1]
    first = lax.psum_scatter(
        term.astype(jnp.bfloat16), "seq", scatter_dimension=0, tiled=True
    )
    ctx_total = lax.axis_size("ctx")
    own = first.shape[0] // ctx_total
    padded = -(-own // 16) * 16
    if padded != own:
        first = first.reshape(ctx_total, own, columns)
        first = jnp.pad(first, ((0, 0), (0, padded - own), (0, 0)))
        first = first.reshape(ctx_total * padded, columns)
    second = lax.psum_scatter(first, "ctx", scatter_dimension=0, tiled=True)
    return second[:own].astype(jnp.float32)


def per_device(
    inputs,
    positions,
    attention_gain,
    query_weight,
    key_weight,
    value_weight,
    query_gain,
    key_gain,
    output_weight,
    attention_post,
    feedfwd_gain,
    gate_weight,
    up_weight,
    down_weight,
    feedfwd_post,
    cotangent,
):
    seq_total = lax.axis_size("seq")
    ctx_total = lax.axis_size("ctx")
    device_total = seq_total * ctx_total
    token_count = inputs.shape[0]
    width_rows = query_weight.shape[0]
    head_rows = query_gain.shape[0]
    unit_rows = down_weight.shape[0]
    scaling = 1.0 / math.sqrt(DH)

    block_number = (positions[:1] // token_count).astype(jnp.bfloat16)
    small = jnp.concatenate(
        [attention_gain, attention_post, feedfwd_gain, feedfwd_post, query_gain, key_gain]
        + [block_number]
    )
    small_row = jnp.pad(small, (0, (H + 2) * DH - small.shape[0]))[None]
    packet = jnp.concatenate(
        [jnp.concatenate([query_weight, key_weight, value_weight], axis=1), small_row], axis=0
    )
    packets = lax.all_gather(packet, BOTH, axis=0, tiled=False)
    joint_weight = packets[:, :width_rows].reshape(D, (H + 2) * DH)
    smalls = packets[:, width_rows]

    def gain_of(start, size):
        return smalls[:, start : start + size].reshape(-1).astype(jnp.float32)

    gain_attention = gain_of(0, width_rows)
    gain_post = gain_of(width_rows, width_rows)
    gain_feed = gain_of(2 * width_rows, width_rows)
    gain_final = gain_of(3 * width_rows, width_rows)
    gain_query = gain_of(4 * width_rows, head_rows)
    gain_key = gain_of(4 * width_rows + head_rows, head_rows)
    numbers = smalls[:, 4 * width_rows + 2 * head_rows].astype(jnp.int32)
    own_numbers = lax.dynamic_slice(numbers, (lax.axis_index("seq") * ctx_total,), (ctx_total,))
    place_all = (
        own_numbers[:, None] * token_count + jnp.arange(token_count, dtype=jnp.int32)[None, :]
    ).reshape(-1)

    pair = jnp.stack([gate_weight, up_weight]).reshape(
        2, width_rows, seq_total, ctx_total, unit_rows
    )
    pair = jnp.transpose(pair, (3, 0, 1, 2, 4)).reshape(
        ctx_total, 2, width_rows, seq_total * unit_rows
    )
    pair = lax.all_to_all(pair, "ctx", 0, 0, tiled=False)
    unit_count = seq_total * unit_rows
    pair = jnp.transpose(pair, (1, 0, 2, 3)).reshape(2 * ctx_total * width_rows, unit_count)

    input_wide = inputs.astype(jnp.float32)
    input_factor = rms_factor(input_wide)
    normed = (input_wide * input_factor * gain_attention).astype(jnp.bfloat16)
    joint = times_right(normed, joint_weight)
    queries = to_heads(joint[:, : H * DH])
    key_rows = joint[:, H * DH : (H + 1) * DH]
    value_rows = joint[:, (H + 1) * DH :].astype(jnp.bfloat16)
    cosine, sinus = rotary(positions)
    cosine_heads = jnp.concatenate([cosine] * H, axis=0)
    sinus_heads = jnp.concatenate([sinus] * H, axis=0)
    query_factor = rms_factor(queries)
    query_rot = rotate(queries * query_factor * gain_query, cosine_heads, sinus_heads).astype(
        jnp.bfloat16
    )
    key_factor = rms_factor(key_rows)
    key_rot = rotate(key_rows * key_factor * gain_key, cosine, sinus).astype(jnp.bfloat16)
    both_rows = lax.all_gather(
        jnp.concatenate([key_rot, value_rows], axis=1), "ctx", axis=0, tiled=True
    )
    output_all = lax.all_gather(output_weight, BOTH, axis=0, tiled=True)
    both_rows, pair, down_own = lax.optimization_barrier((both_rows, pair, down_weight))
    pair_all = lax.all_gather(pair, "seq", axis=0, tiled=True).reshape(
        seq_total, 2, ctx_total * width_rows, unit_count
    )
    gate_all = pair_all[:, 0].reshape(D, unit_count)
    up_all = pair_all[:, 1].reshape(D, unit_count)
    down_all = lax.all_gather(down_own, "seq", axis=0, tiled=True)

    key_all = both_rows[:, :DH]
    value_all = both_rows[:, DH:]
    place_heads = jnp.concatenate([positions] * H, axis=0)
    allowed = place_all[None, :] <= place_heads[:, None]
    scores = times_transposed(query_rot, key_all) * scaling
    expscore = jnp.where(allowed, jnp.exp(scores), 0.0)
    weight_sum = jnp.sum(expscore, axis=-1, keepdims=True)
    summed = times_right(expscore.astype(jnp.bfloat16), value_all)
    attended_heads = (summed / weight_sum).astype(jnp.bfloat16)
    logsum = jnp.log(weight_sum)
    attended = from_heads(attended_heads)
    mixed_values = times_right(attended, output_all)
    mixed_factor = rms_factor(mixed_values)
    residual = input_wide + mixed_values * mixed_factor * gain_post
    residual_factor = rms_factor(residual)
    fed_own = (residual * residual_factor * gain_feed).astype(jnp.bfloat16)

    fed_rows = lax.all_gather(fed_own, "ctx", axis=0, tiled=True)
    gate_values = times_right(fed_rows, gate_all)
    up_values = times_right(fed_rows, up_all)
    hidden = (gelu_tanh(gate_values) * up_values).astype(jnp.bfloat16)
    down_values = lax.psum_scatter(
        times_right(hidden, down_all).astype(jnp.bfloat16), "ctx", scatter_dimension=0, tiled=True
    ).astype(jnp.float32)
    down_factor = rms_factor(down_values)
    block_out = (residual + down_values * down_factor * gain_final).astype(jnp.bfloat16)
    cot_wide = cotangent.astype(jnp.float32)
    grad_final = jnp.sum(cot_wide * down_values * down_factor, axis=0)
    down_back_own = norm_back(down_values, down_factor, gain_final, cot_wide).astype(jnp.bfloat16)
    down_back = lax.all_gather(down_back_own, "ctx", axis=0, tiled=True)
    hidden_back = times_transposed(down_back, down_all)
    gate_back = (hidden_back * up_values * gelu_slope(gate_values)).astype(jnp.bfloat16)
    up_back = (hidden_back * gelu_tanh(gate_values)).astype(jnp.bfloat16)
    fed_back = lax.psum_scatter(
        (times_transposed(gate_back, gate_all) + times_transposed(up_back, up_all)).astype(
            jnp.bfloat16
        ),
        "ctx",
        scatter_dimension=0,
        tiled=True,
    ).astype(jnp.float32)
    fed_back, late_hidden, late_down, late_fed, late_gate, late_up = lax.optimization_barrier(
        (fed_back, hidden, down_back, fed_rows, gate_back, up_back)
    )
    grad_down = lax.psum_scatter(
        transposed_times(late_hidden, late_down).astype(jnp.bfloat16),
        "seq",
        scatter_dimension=0,
        tiled=True,
    ).astype(jnp.float32)
    seq_rows = ctx_total * width_rows
    pair_term = jnp.stack(
        [
            transposed_times(late_fed, late_gate).astype(jnp.bfloat16).reshape(
                seq_total, seq_rows, unit_count
            ),
            transposed_times(late_fed, late_up).astype(jnp.bfloat16).reshape(
                seq_total, seq_rows, unit_count
            ),
        ],
        axis=1,
    ).reshape(seq_total * 2 * seq_rows, unit_count)
    pair_sum = lax.psum_scatter(pair_term, "seq", scatter_dimension=0, tiled=True)

    grad_feed = jnp.sum(fed_back * residual * residual_factor, axis=0)
    residual_back = cot_wide + norm_back(residual, residual_factor, gain_feed, fed_back)
    grad_post = jnp.sum(residual_back * mixed_values * mixed_factor, axis=0)
    mixed_back = norm_back(mixed_values, mixed_factor, gain_post, residual_back).astype(
        jnp.bfloat16
    )
    attended_back = to_heads(times_transposed(mixed_back, output_all))
    upper_round = attended_back.astype(jnp.bfloat16)
    row_delta = jnp.sum(attended_back * attended_heads.astype(jnp.float32), axis=-1, keepdims=True)
    probability = jnp.where(allowed, jnp.exp(scores - logsum), 0.0)
    value_terms = transposed_times(probability.astype(jnp.bfloat16), upper_round)
    prob_back = times_transposed(upper_round, value_all)
    score_back = (probability * (prob_back - row_delta) * scaling).astype(jnp.bfloat16)
    query_rot_back = times_right(score_back, key_all)
    key_terms = transposed_times(score_back, query_rot)
    own_rows = lax.psum_scatter(
        jnp.concatenate([key_terms, value_terms], axis=1).astype(jnp.bfloat16),
        "ctx",
        scatter_dimension=0,
        tiled=True,
    ).astype(jnp.float32)
    grad_output = sum_to_owner(transposed_times(attended, mixed_back))
    key_rot_back = own_rows[:, :DH]
    value_back = own_rows[:, DH:].astype(jnp.bfloat16)
    query_up = rotate_back(query_rot_back, cosine_heads, sinus_heads)
    grad_qgain = jnp.sum(query_up * queries * query_factor, axis=0)
    query_back = from_heads(
        norm_back(queries, query_factor, gain_query, query_up).astype(jnp.bfloat16)
    )
    key_up = rotate_back(key_rot_back, cosine, sinus)
    grad_kgain = jnp.sum(key_up * key_rows * key_factor, axis=0)
    key_back = norm_back(key_rows, key_factor, gain_key, key_up).astype(jnp.bfloat16)
    joint_back = jnp.concatenate([query_back, key_back, value_back], axis=1)
    normed_back = times_transposed(joint_back, joint_weight)
    grad_attention = jnp.sum(normed_back * input_wide * input_factor, axis=0)
    input_grad = residual_back + norm_back(input_wide, input_factor, gain_attention, normed_back)
    grad_joint = sum_to_owner(transposed_times(normed, joint_back))
    grad_query = grad_joint[:, : H * DH]
    grad_key = grad_joint[:, H * DH : (H + 1) * DH]
    grad_value = grad_joint[:, (H + 1) * DH :]
    pair_back = jnp.transpose(
        pair_sum.reshape(2, ctx_total, width_rows, unit_count), (1, 0, 2, 3)
    )
    pair_back = lax.all_to_all(pair_back, "ctx", 0, 0, tiled=False)
    pair_back = jnp.transpose(
        pair_back.reshape(ctx_total, 2, width_rows, seq_total, unit_rows), (1, 2, 3, 0, 4)
    ).reshape(2, width_rows, FF)
    grad_gate = pair_back[0].astype(jnp.float32)
    grad_up = pair_back[1].astype(jnp.float32)
    gains_summed = tuple(
        lax.psum_scatter(term, BOTH, scatter_dimension=0, tiled=True)
        for term in (grad_attention, grad_qgain, grad_kgain, grad_post, grad_feed, grad_final)
    )
    return (
        block_out,
        input_grad,
        gains_summed[0],
        grad_query,
        grad_key,
        grad_value,
        gains_summed[1],
        gains_summed[2],
        grad_output,
        gains_summed[3],
        gains_summed[4],
        grad_gate,
        grad_up,
        grad_down,
        gains_summed[5],
    )


def solution(mesh):
    return jax.shard_map(
        per_device,
        mesh=mesh,
        in_specs=(
            P(("seq", "ctx"), None),
            P(("seq", "ctx")),
            P(("seq", "ctx")),
            P(("seq", "ctx"), None),
            P(("seq", "ctx"), None),
            P(("seq", "ctx"), None),
            P(("seq", "ctx")),
            P(("seq", "ctx")),
            P(("seq", "ctx"), None),
            P(("seq", "ctx")),
            P(("seq", "ctx")),
            P(("seq", "ctx"), None),
            P(("seq", "ctx"), None),
            P(("seq", "ctx"), None),
            P(("seq", "ctx")),
            P(("seq", "ctx"), None),
        ),
        out_specs=(
            P(("seq", "ctx"), None),
            P(("seq", "ctx"), None),
            P(("seq", "ctx")),
            P(("seq", "ctx"), None),
            P(("seq", "ctx"), None),
            P(("seq", "ctx"), None),
            P(("seq", "ctx")),
            P(("seq", "ctx")),
            P(("seq", "ctx"), None),
            P(("seq", "ctx")),
            P(("seq", "ctx")),
            P(("seq", "ctx"), None),
            P(("seq", "ctx"), None),
            P(("seq", "ctx"), None),
            P(("seq", "ctx")),
        ),
        check_vma=False,
    )
```
